32 devices in a mesh: grp: 4 (over z), run: 2 (over y), head: 4 (over x, core).
Axes of the slice: x: 2, y: 2, z: 4, core: 2. Of those that a mesh axis runs over, the one named last changes fastest.
Arguments:
- queries: bfloat16 [2, 16384, 2048], P(None, ('grp', 'run'), 'head'), may hold values from -6 to 6
- keys: bfloat16 [2, 16384, 2048], P(None, ('grp', 'run'), 'head'), may hold values from -30 to 30
- values: bfloat16 [2, 16384, 2048], P(None, ('grp', 'run'), 'head'), may hold values from -6 to 6
- forget_exponent: float32 [2, 16, 16384], P(None, 'head', ('grp', 'run')), may hold values from -2 to 0
- beta: float32 [2, 16, 16384], P(None, 'head', ('grp', 'run')), may hold values from 0 to 0.9
- lengths: int32 [2], replicated, may hold values from 8192 to 16384, as said below
- norm_gain: float32 [128], replicated, may hold values from 0.1 to 1.9
Outputs:
- normed_out: bfloat16 [2, 16384, 2048], P(None, ('grp', 'run', 'head'))
- final_state: float32 [2, 16, 128, 128], P(None, 'head', ('grp', 'run'))
The draws below stay inside these ranges and needn't reach their ends.
Inputs may be any that keep to these rules, and one draw needn't show every extreme that they name: `lengths`: one history always uses all 16384 positions.
All inputs are finite; a program needn't handle non-finite values.
Results may differ from the reference program's by a relative error of at most 0.0061.
Values may be sent and summed in bfloat16 or wider, within the bound.
No kernel may reach another device: no remote copies, remote signals or barrier semaphores. Data moves between devices by JAX's collectives and lax.ppermute only.
A program may use at most 320 MiB of HBM per device.

```python
import math
import jax
import jax.numpy as jnp
from jax import lax

ATTENTION_COUNT = 16
DK = 128
DV = 128
RECORD_COUNT = 2
TOK_DEV = 2048
VISIT_COUNT = 16384


def gate_law(key):
    key = jax.random.fold_in(key, 41)
    stochastic_seeds = jax.random.split(key, 9)
    slow_share = 0.5
    chooser = jax.random.uniform(stochastic_seeds[0], (RECORD_COUNT, ATTENTION_COUNT, 1), jnp.float32)
    slow_rate = jnp.exp(jax.random.uniform(stochastic_seeds[1], (RECORD_COUNT, ATTENTION_COUNT, 1), jnp.float32, math.log(0.2), math.log(0.7))) / VISIT_COUNT
    middle_rate = jnp.exp(jax.random.uniform(stochastic_seeds[2], (RECORD_COUNT, ATTENTION_COUNT, 1), jnp.float32, math.log(1.0 / TOK_DEV), math.log(1.0 / 50.0)))
    fast_rate = jnp.exp(jax.random.uniform(stochastic_seeds[3], (RECORD_COUNT, ATTENTION_COUNT, 1), jnp.float32, math.log(1.0 / 50.0), math.log(1.0 / 30.0)))
    channel_speed = jnp.where(chooser < slow_share, slow_rate, jnp.where(chooser < slow_share + (1.0 - slow_share) * 0.5, middle_rate, fast_rate))
    noise_amplitude = jnp.exp(jax.random.uniform(stochastic_seeds[4], (RECORD_COUNT, ATTENTION_COUNT, VISIT_COUNT), jnp.float32, -math.log(2.0), math.log(2.0)))
    shard_factor = jnp.exp(jax.random.uniform(stochastic_seeds[5], (RECORD_COUNT, ATTENTION_COUNT, VISIT_COUNT // TOK_DEV, 1), jnp.float32, -math.log(2.0), math.log(2.0)))
    noise_amplitude = noise_amplitude * jnp.broadcast_to(shard_factor, (RECORD_COUNT, ATTENTION_COUNT, VISIT_COUNT // TOK_DEV, TOK_DEV)).reshape(RECORD_COUNT, ATTENTION_COUNT, VISIT_COUNT)
    spike_position = jax.random.randint(stochastic_seeds[6], (RECORD_COUNT, ATTENTION_COUNT, 2), 0, VISIT_COUNT)
    sudden_drop = jnp.log(jax.random.uniform(stochastic_seeds[7], (RECORD_COUNT, ATTENTION_COUNT, 2), jnp.float32, 0.5, 0.8))
    spike_indicator = jnp.arange(VISIT_COUNT, dtype=jnp.int32)[None, None, None, :] == spike_position[..., None]
    spike_instances = jnp.sum(jnp.where(spike_indicator, sudden_drop[..., None], 0.0), axis=2)
    forget_exponent = -channel_speed * noise_amplitude + spike_instances
    beta_spread = jax.random.uniform(stochastic_seeds[8], (RECORD_COUNT, ATTENTION_COUNT, VISIT_COUNT), jnp.float32, 0.6, 1.0)
    beta = jnp.minimum(0.9, 0.5 * DK * channel_speed) * beta_spread
    return (forget_exponent, beta)


def draw_forget_exponent(key, part):
    return gate_law(key)[0]


def draw_beta(key, part):
    return gate_law(key)[1]


def draw_keys(key, part):
    key = jax.random.fold_in(key, 17)
    first, second, third = jax.random.split(key, 3)
    signs = jax.random.randint(third, (RECORD_COUNT, 1, ATTENTION_COUNT, DK), 0, 2)
    direction = 2.0 * signs.astype(jnp.float32) - 1.0
    noise = jnp.clip(jax.random.normal(first, (RECORD_COUNT, VISIT_COUNT, ATTENTION_COUNT, DK), jnp.float32), -6.0, 6.0)
    row_scale = jnp.exp(jax.random.uniform(second, (RECORD_COUNT, VISIT_COUNT, ATTENTION_COUNT, 1), jnp.float32, math.log(0.5), math.log(5.0)))
    entries = 0.8 * direction + 0.6 * noise
    return jnp.clip(entries * row_scale, -30.0, 30.0).reshape(RECORD_COUNT, VISIT_COUNT, ATTENTION_COUNT * DK).astype(jnp.bfloat16)


def draw_lengths(key, part):
    key = jax.random.fold_in(key, 3)
    first, second = jax.random.split(key)
    shorter = jax.random.randint(first, (), VISIT_COUNT // 2, VISIT_COUNT + 1)
    full_index = jax.random.randint(second, (), 0, RECORD_COUNT)
    return jnp.where(jnp.arange(RECORD_COUNT) == full_index, VISIT_COUNT, shorter).astype(jnp.int32)


def shard_levels(key, dims, shards, least, high):
    def one(dim, parts):
        heights = jax.random.uniform(jax.random.fold_in(jax.random.fold_in(key, 6), dim), (parts,), jnp.float32, least / len(shards), high / len(shards))
        return jnp.repeat(jnp.exp(heights), dims[dim] // parts).reshape((-1,) + (1,) * (len(dims) - dim - 1))

    level = one(*shards[0])
    for cut in shards[1:]:
        level = level * one(*cut)
    return level


def normal_values(own_key, extent, width, bound, cuts=(), held_as=jnp.bfloat16):
    values = width * jax.random.normal(own_key, extent, jnp.float32)
    if cuts:
        values = values * shard_levels(own_key, extent, cuts, -0.22, 0.18)
    return jnp.clip(values, -bound, bound).astype(held_as)


def setup_inputs(seed: int = 0) -> dict:
    arg_keys = jax.random.split(jax.random.key(seed), 8)
    queries = normal_values(arg_keys[0], (RECORD_COUNT, VISIT_COUNT, ATTENTION_COUNT * DK), 1.0, 6.0, ((1, 8), (2, 4)))
    keys = draw_keys(jax.random.fold_in(arg_keys[7], 71), 0)
    values = normal_values(arg_keys[2], (RECORD_COUNT, VISIT_COUNT, ATTENTION_COUNT * DV), 1.0, 6.0, ((1, 8), (2, 4)))
    forget_exponent = draw_forget_exponent(jax.random.fold_in(arg_keys[7], 71), 0)
    beta = draw_beta(jax.random.fold_in(arg_keys[7], 71), 0)
    lengths = draw_lengths(jax.random.fold_in(arg_keys[7], 71), 0)
    norm_gain = jnp.clip(1.0 + 0.18 * jax.random.normal(arg_keys[6], (DV,), jnp.float32), 0.1, 1.9)
    return {"queries": queries, "keys": keys, "values": values, "forget_exponent": forget_exponent, "beta": beta, "lengths": lengths, "norm_gain": norm_gain}


highest = lax.Precision.HIGHEST

def reference(queries, keys, values, forget_exponent, beta, lengths, norm_gain):
    key_float = keys.astype(jnp.float32).reshape(RECORD_COUNT, VISIT_COUNT, ATTENTION_COUNT, DK)
    key_unit = (key_float / jnp.sqrt(lax.optimization_barrier(jnp.sum(key_float * key_float, axis=-1, keepdims=True)) + 1e-06)).astype(jnp.bfloat16)
    key_unit = lax.optimization_barrier(key_unit)
    position = jnp.arange(VISIT_COUNT, dtype=jnp.int32)
    valid_rows = position[None, :] < lengths[:, None]
    decay = jnp.exp(jnp.where(valid_rows[:, None, :], forget_exponent, 0.0))
    update_rates = jnp.where(valid_rows[:, None, :], beta, 0.0)
    inputs = (queries.reshape(RECORD_COUNT, VISIT_COUNT, ATTENTION_COUNT, DK).transpose(1, 0, 2, 3), key_unit.transpose(1, 0, 2, 3), values.reshape(RECORD_COUNT, VISIT_COUNT, ATTENTION_COUNT, DV).transpose(1, 0, 2, 3), decay.transpose(2, 0, 1), update_rates.transpose(2, 0, 1), valid_rows.transpose(1, 0))

    def advance(state, step_inputs):
        query_now, key_now, value_now, decay_now, rate_now, valid_now = step_inputs
        query_float = query_now.astype(jnp.float32)
        key_vector = key_now.astype(jnp.float32)
        value_float = value_now.astype(jnp.float32)
        recalled = jnp.einsum('nhvd,nhd->nhv', state, key_vector, precision=highest)
        kept = state - (rate_now[..., None] * recalled)[..., None] * key_vector[..., None, :]
        state = decay_now[..., None, None] * kept + (rate_now[..., None] * value_float)[..., None] * key_vector[..., None, :]
        readout = jnp.einsum('nhvd,nhd->nhv', state, query_float, precision=highest)
        normed = readout / jnp.sqrt(lax.optimization_barrier(jnp.mean(readout * readout, axis=-1, keepdims=True)) + 1e-06) * norm_gain
        normed = jnp.where(valid_now[:, None, None], normed, 0.0).astype(jnp.bfloat16)
        return (state, normed)
    start_state = jnp.zeros((RECORD_COUNT, ATTENTION_COUNT, DV, DK), jnp.float32)
    final_state, normed = lax.scan(advance, start_state, inputs)
    normed_out = normed.transpose(1, 0, 2, 3).reshape(RECORD_COUNT, VISIT_COUNT, ATTENTION_COUNT * DV)
    return (normed_out, final_state)
```

```python
import jax
import jax.numpy as jnp
from jax import lax
from jax.experimental import pallas as pl
from jax.experimental.pallas import tpu as pltpu
from jax.sharding import PartitionSpec as P

C = 128
SMALL = 16
f32 = jnp.float32
bf16 = jnp.bfloat16
MAP = bf16


def mm(a, b):
    return jnp.dot(a, b, preferred_element_type=f32)


def mm_nt(a, b):
    return lax.dot_general(a, b, (((1,), (1,)), ((), ())), preferred_element_type=f32)


def split(x):
    hi = x.astype(bf16)
    return hi, (x - hi.astype(f32)).astype(bf16)


def mm3(a, b):
    ah, al = split(a)
    bh, bl = split(b)
    return mm(jnp.concatenate([ah, al], axis=1), jnp.concatenate([bh, bh], axis=0)) + mm(ah, bl)


def iota(shape, axis):
    return lax.broadcasted_iota(jnp.int32, shape, axis)


def unit_lower_inverse(ns, product):
    lane = iota((SMALL, C), 1)
    first = lane // SMALL * SMALL
    packed = []
    for n in ns:
        p = jnp.zeros((SMALL, C), f32)
        for r in range(C // SMALL):
            p = jnp.where(lane // SMALL == r, n[r * SMALL:(r + 1) * SMALL, :], p)
        packed.append(p)
    ts = [(lane - first == iota((SMALL, C), 0)).astype(f32) for _ in ns]
    for j in range(SMALL - 1):
        columns = [jnp.take_along_axis(p, first + j, axis=1) for p in packed]
        ts = [t - c * t[j:j + 1, :] for t, c in zip(ts, columns)]
    ts = [jnp.concatenate(
        [jnp.where(lane // SMALL == r, t, 0.0) for r in range(C // SMALL)], axis=0) for t in ts]
    size = SMALL
    while size < C:
        lane_block = iota((size, C), 1) // size
        starts = range(size, C, 2 * size)
        lows = [jnp.concatenate(
            [jnp.where(lane_block == 2 * i, n[s:s + size], 0.0) for i, s in enumerate(starts)],
            axis=0) for n in ns]
        ys = [product(low, t) for low, t in zip(lows, ts)]
        zero = jnp.zeros((size, C), f32)
        ys = [jnp.concatenate(
            [z for i in range(len(starts)) for z in (zero, y[i * size:(i + 1) * size])], axis=0)
            for y in ys]
        t_lows = [jnp.concatenate([t[s:s + size] for s in starts], axis=0) for t in ts]
        t_lows = [t - product(t, y) for t, y in zip(t_lows, ys)]
        ts = [jnp.concatenate(
            [z for i, s in enumerate(starts)
             for z in (t[s - size:s], low[i * size:(i + 1) * size])], axis=0)
            for t, low in zip(ts, t_lows)]
        size *= 2
    return ts


def prepare(qs, ks, cums, rates):
    kfs = [k.astype(f32) for k in ks]
    kbs = [(kf * lax.rsqrt(jnp.sum(kf * kf, axis=1, keepdims=True) + 1e-6)).astype(bf16) for kf in kfs]
    kts = [kb.T for kb in kbs]
    inners = [mm(jnp.concatenate([kb, q], axis=0), kt) for kb, q, kt in zip(kbs, qs, kts)]
    row, col = iota((C, C), 0), iota((C, C), 1)
    ns, attends, khs, kls, growths, ends = [], [], [], [], [], []
    for cum, rate, inner, kt in zip(cums, rates, inners, kts):
        cr = jnp.broadcast_to(cum, (C, C))
        cc = cr.T
        spread = jnp.exp(jnp.where(row >= col, cc - cr, -1e30)) * rate
        ns.append(jnp.where(row > col, inner[:C] * spread, 0.0))
        attends.append((inner[C:] * spread).astype(bf16))
        end = cum[:, C - 1:C]
        growths.append(jnp.exp(cc))
        kh, kl = split(kt.astype(f32) * (rate * jnp.exp(end - cum)))
        khs.append(kh)
        kls.append(kl)
        ends.append(jnp.exp(end))
    ts = [t.astype(bf16) for t in unit_lower_inverse(ns, mm3)]
    return list(zip(kbs, ts, attends, khs, kls, growths, ends))


def advance(xs, qs, vs, preps):
    seens, growths = [], []
    for x, q, prep in zip(xs, qs, preps):
        qk = jnp.concatenate([prep[0], q], axis=0)
        seens.append(mm(jnp.concatenate([qk, qk], axis=1), jnp.concatenate(split(x), axis=0)))
        growths.append(jnp.concatenate([prep[5], prep[5]], axis=1))
    freshs = []
    for seen, growth, v, prep in zip(seens, growths, vs, preps):
        scaled = growth * seen[:C]
        rest = jnp.concatenate([v.astype(f32) - scaled[:, :C], -scaled[:, C:]], axis=1)
        t = prep[1]
        freshs.append(mm(jnp.concatenate([t, t], axis=1), jnp.concatenate(split(rest), axis=0)))
    news, outs = [], []
    for x, seen, growth, fresh, prep in zip(xs, seens, growths, freshs, preps):
        kb, t, attend, kh, kl, _, end = prep
        left = jnp.concatenate(
            [jnp.concatenate([attend, attend], axis=1), jnp.concatenate([kh, kh], axis=1),
             jnp.concatenate([kl, jnp.zeros_like(kl)], axis=1)], axis=0)
        got = mm(left, jnp.concatenate(split(fresh), axis=0))
        outs.append(growth * seen[C:] + got[:C])
        news.append(x * end + (got[C:2 * C] + got[2 * C:]))
    return news, outs


def cumulate(g):
    low = (iota((C, C), 0) <= iota((C, C), 1)).astype(f32)
    pad = jnp.concatenate([g, jnp.zeros((8 - g.shape[0], C), f32)], axis=0) if g.shape[0] < 8 else g
    return jnp.dot(pad, low, precision=lax.Precision.HIGHEST, preferred_element_type=f32)


def local_kernel(length_ref, q_ref, k_ref, v_ref, g_ref, b_ref, o_ref, e_ref, map_ref, x_ref):
    heads = g_ref.shape[1]
    step = pl.program_id(1)
    eye = (iota((C, C), 0) == iota((C, C), 1)).astype(f32)

    @pl.when(step == 0)
    def _():
        for h in range(heads):
            x_ref[h] = jnp.concatenate([jnp.zeros((C, C), f32), eye], axis=1)

    valid = step * C + iota((heads, C), 1) < length_ref[pl.program_id(0)]
    cum = cumulate(jnp.where(valid, g_ref[0], 0.0))
    rate = jnp.where(valid, b_ref[0], 0.0)
    parts = [slice(h * C, (h + 1) * C) for h in range(heads)]
    qs = [q_ref[0, :, part] for part in parts]
    preps = prepare(qs, [k_ref[0, :, part] for part in parts],
                    [cum[h:h + 1] for h in range(heads)], [rate[h:h + 1] for h in range(heads)])
    xs, outs = advance([x_ref[h] for h in range(heads)], qs, [v_ref[0, :, part] for part in parts], preps)
    for h, part in enumerate(parts):
        x_ref[h] = xs[h]
        o_ref[0, :, part] = outs[h][:, :C].astype(o_ref.dtype)
        e_ref[0, :, part] = outs[h][:, C:].astype(e_ref.dtype)

    @pl.when(step == pl.num_programs(1) - 1)
    def _():
        for h in range(heads):
            map_ref[0, h, :C] = x_ref[h, :, :C].T.astype(map_ref.dtype)
            map_ref[0, h, C:] = x_ref[h, :, C:].T.astype(map_ref.dtype)


def local_pass(length, q, k, v, g, b):
    n, tokens, width = q.shape
    heads = g.shape[1]
    wide = pl.BlockSpec((1, C, width), lambda i, t, _: (i, t, 0))
    gate = pl.BlockSpec((1, heads, C), lambda i, t, _: (i, 0, t))
    maps = pl.BlockSpec((1, heads, 2 * C, C), lambda i, t, _: (i, 0, 0, 0))
    return pl.pallas_call(
        local_kernel,
        grid_spec=pltpu.PrefetchScalarGridSpec(
            num_scalar_prefetch=1, grid=(n, tokens // C),
            in_specs=[wide, wide, wide, gate, gate],
            out_specs=[wide, wide, maps],
            scratch_shapes=[pltpu.VMEM((heads, C, 2 * C), f32)]),
        out_shape=[
            jax.ShapeDtypeStruct(q.shape, bf16),
            jax.ShapeDtypeStruct(q.shape, bf16),
            jax.ShapeDtypeStruct((n, heads, 2 * C, C), MAP)],
        compiler_params=pltpu.CompilerParams(dimension_semantics=("arbitrary", "arbitrary")),
        name="local_pass",
    )(length, q, k, v, g, b)


def prefix_kernel(map_ref, start_ref, final_ref):
    count, rows = start_ref.shape[:2]
    own = final_ref.shape[1]
    state = jnp.zeros((rows, C), f32)
    for i in range(count):
        start_ref[i] = state.astype(start_ref.dtype)
        step = map_ref[i, rows:].astype(f32)
        state = mm3(state, step) + map_ref[i, :rows].astype(f32)
    for i in range(count):
        first = i * own % rows
        final_ref[i] = state[first:first + own]


def prefix_pass(maps):
    count, rows, _ = maps.shape
    return pl.pallas_call(
        prefix_kernel,
        out_shape=[
            jax.ShapeDtypeStruct((count, rows - C, C), MAP),
            jax.ShapeDtypeStruct((count, C // count, C), f32)],
        name="prefix_pass",
    )(maps)


def output_kernel(length_ref, o_ref, e_ref, start_ref, gain_ref, out_ref):
    rows = o_ref.shape[1]
    position = pl.program_id(1) * rows + iota((rows, C), 0)
    valid = position < length_ref[pl.program_id(0)]
    gain = gain_ref[...]
    for h in range(start_ref.shape[1]):
        part = slice(h * C, (h + 1) * C)
        o = o_ref[0, :, part].astype(f32) + mm_nt(e_ref[0, :, part], start_ref[0, h])
        scale = lax.rsqrt(jnp.mean(o * o, axis=1, keepdims=True) + 1e-6)
        out_ref[0, 0, :, part] = jnp.where(valid, o * scale * gain, 0.0).astype(out_ref.dtype)


def output_pass(length, o, e, starts, gain, parts):
    n, tokens, width = o.shape
    heads = starts.shape[1]
    rows = tokens // parts
    wide = pl.BlockSpec((1, rows, width), lambda i, t, _: (i, t, 0))
    return pl.pallas_call(
        output_kernel,
        grid_spec=pltpu.PrefetchScalarGridSpec(
            num_scalar_prefetch=1, grid=(n, parts),
            in_specs=[wide, wide,
                      pl.BlockSpec((1, heads, C, C), lambda i, t, _: (i, 0, 0, 0)),
                      pl.BlockSpec((1, C), lambda i, t, _: (0, 0))],
            out_specs=pl.BlockSpec((1, 1, rows, width), lambda i, t, _: (t, i, 0, 0))),
        out_shape=jax.ShapeDtypeStruct((parts, n, rows, width), bf16),
        compiler_params=pltpu.CompilerParams(dimension_semantics=("arbitrary", "arbitrary")),
        name="output_pass",
    )(length, o, e, starts, gain)


def shards(queries, keys, values, forget_exponent, beta, lengths, norm_gain):
    n, tokens, width = queries.shape
    heads = forget_exponent.shape[1]
    pairs = n * heads
    times = ("grp", "run")
    count = lax.axis_size("grp") * lax.axis_size("run")
    mine = lax.axis_index("grp") * lax.axis_size("run") + lax.axis_index("run")
    owners = count // pairs
    length = lengths - mine * tokens
    o, e, maps = local_pass(length, queries, keys, values, forget_exponent, beta)
    maps = maps.reshape(pairs, 2 * C, C)
    rows = C // owners
    if owners > 1:
        shift = maps[:, :C].reshape(count, rows, C)
        move = jnp.broadcast_to(maps[:, None, C:], (pairs, owners, C, C)).reshape(count, C, C)
        maps = jnp.concatenate([shift, move], axis=1)
    maps = lax.all_to_all(maps, times, 0, 0, tiled=True)
    starts, finals = prefix_pass(maps)
    starts = lax.all_to_all(starts, times, 0, 0, tiled=True).reshape(n, heads, C, C)
    finals = lax.all_to_all(finals, times, 0, 0, tiled=True)
    own = C // count
    finals = finals.reshape(pairs, owners, own, C)
    finals = lax.dynamic_index_in_dim(finals, mine * own // rows, 1, keepdims=False)
    parts = lax.axis_size("head")
    out = output_pass(length, o, e, starts, norm_gain[None], parts)
    out = lax.all_to_all(out, "head", 0, 0, tiled=True)
    out = out.transpose(1, 2, 0, 3).reshape(n, tokens // parts, parts * width)
    return out, finals.reshape(n, heads, own, C)


def solution(mesh):
    wide = P(None, ("grp", "run"), "head")
    gate = P(None, "head", ("grp", "run"))
    return jax.shard_map(
        shards,
        mesh=mesh,
        in_specs=(wide, wide, wide, gate, gate, P(), P()),
        out_specs=(P(None, ("grp", "run", "head"), None), P(None, "head", ("grp", "run"), None)),
        check_vma=False,
    )
```

```python
import jax
import jax.numpy as jnp
from jax import lax
from jax.experimental import pallas as pl
from jax.experimental.pallas import tpu as pltpu
from jax.sharding import PartitionSpec as P

C = 128
SMALL = 16
f32 = jnp.float32
bf16 = jnp.bfloat16
MAP = bf16
PACE = 2.0
CHUNKS = 2


def mm(a, b):
    return jnp.dot(a, b, preferred_element_type=f32)


def mm_nt(a, b):
    return lax.dot_general(a, b, (((1,), (1,)), ((), ())), preferred_element_type=f32)


def split(x):
    hi = x.astype(bf16)
    return hi, (x - hi.astype(f32)).astype(bf16)


def mm3(a, b):
    ah, al = split(a)
    bh, bl = split(b)
    return mm(jnp.concatenate([ah, al], axis=1), jnp.concatenate([bh, bh], axis=0)) + mm(ah, bl)


def iota(shape, axis):
    return lax.broadcasted_iota(jnp.int32, shape, axis)


def rows(parts):
    return jnp.concatenate(parts, axis=0)


def lanes(parts):
    return jnp.concatenate(parts, axis=1)


def cumulate(g):
    low = (iota((C, C), 0) <= iota((C, C), 1)).astype(f32)
    pad = -g.shape[0] % 8
    if pad:
        g = rows([g, jnp.zeros((pad, C), f32)])
    return jnp.dot(g, low, precision=lax.Precision.HIGHEST, preferred_element_type=f32)


def prepare(tasks, q_ref, k_ref, g, b, kept):
    cum = cumulate(g)
    qk_ref, t_ref, a_ref, kend_ref, growth_ref, end_ref = kept
    row, col = iota((C, C), 0), iota((C, C), 1)
    kbs = []
    for u, h in tasks:
        kf = k_ref[0, u * C:(u + 1) * C, h * C:(h + 1) * C].astype(f32)
        kbs.append((kf * lax.rsqrt(jnp.sum(kf * kf, axis=1, keepdims=True) + 1e-6)).astype(bf16))
        yield
    kts, qks, inners = [], [], []
    for (u, h), kb in zip(tasks, kbs):
        kts.append(kb.T)
        qks.append(rows([kb, q_ref[0, u * C:(u + 1) * C, h * C:(h + 1) * C]]))
        inners.append(mm(qks[-1], kts[-1]))
        yield
    ns, later = [], []
    for i, (inner, kt, qk) in enumerate(zip(inners, kts, qks)):
        one, rate = cum[i:i + 1], b[i:i + 1]
        cr = jnp.broadcast_to(one, (C, C))
        cc = cr.T
        spread = jnp.exp(jnp.where(row >= col, cc - cr, -1e30)) * rate
        ns.append(jnp.where(row > col, inner[:C] * spread, 0.0))
        end = one[:, C - 1:C]
        kend = split(kt.astype(f32) * (rate * jnp.exp(end - one)))
        later.append((qk, (inner[C:] * spread).astype(bf16), kend, jnp.exp(cc), jnp.exp(end)))
        yield
    lane = iota((SMALL, C), 1)
    first = lane // SMALL * SMALL
    packed = []
    for n in ns:
        p = jnp.zeros((SMALL, C), f32)
        for r in range(C // SMALL):
            p = jnp.where(lane // SMALL == r, n[r * SMALL:(r + 1) * SMALL, :], p)
        packed.append(p)
        yield
    ts = [(lane - first == iota((SMALL, C), 0)).astype(f32) for _ in ns]
    for j in range(SMALL - 1):
        columns = [jnp.take_along_axis(p, first + j, axis=1) for p in packed]
        ts = [t - c * t[j:j + 1, :] for t, c in zip(ts, columns)]
        if j % 2 == 1:
            yield
    size = SMALL
    while size < C:
        block = iota((size, C), 1) // size
        count = C // size
        masks = [block == r for r in range(count)]
        zero = jnp.zeros((size, C), bf16)
        ys, halves = [], []
        for n, t in zip(ns, ts):
            low = jnp.zeros((size, C), f32)
            for r in range(0, count, 2):
                low = jnp.where(masks[r], n[(r + 1) * size:(r + 2) * size, :], low)
            th, tl = split(t)
            right = lanes([rows([z for r in range(0, count, 2)
                                 for z in (jnp.where(masks[r], x, jnp.zeros_like(x)), zero)])
                           for x in (th, tl)])
            got = mm(rows(split(low)), right)
            ys.append(got[:size, :C] + (got[:size, C:] + got[size:, :C]))
            halves.append(rows([th, tl]))
            yield
        news = []
        even = block % 2 == 0
        for y, t, half in zip(ys, ts, halves):
            right = lanes([rows([z for r in range(0, count, 2)
                                 for z in (zero, jnp.where(masks[r], x, jnp.zeros_like(x)))])
                           for x in split(y)])
            got = mm(half, right)
            low = got[:size, :C] + (got[:size, C:] + got[size:, :C])
            news.append(rows([jnp.where(even, t, 0.0), jnp.where(even, -low, t)]))
            yield
        ts = news
        size *= 2
    for i, (t, (qk, attend, kend, growth, end)) in enumerate(zip(ts, later)):
        qk_ref[i] = qk
        t_ref[i] = t.astype(bf16)
        a_ref[i] = attend
        kend_ref[i] = rows(kend)
        growth_ref[i] = growth
        end_ref[i] = jnp.broadcast_to(end, (8, C))


def advance(heads, chunks, v_ref, kept, x_ref, o_ref, e_ref, fresh_start, start):
    qk_ref, t_ref, a_ref, kend_ref, growth_ref, end_ref = kept
    xs = [jnp.where(fresh_start, start[h], x_ref[h]) for h in heads]
    for u in range(chunks):
        slots = [u * len(heads) + h for h in heads]
        seens = []
        for i, x in zip(slots, xs):
            qk = qk_ref[i]
            seens.append(mm(lanes([qk, qk]), rows(split(x))))
            yield
        freshs, growths = [], []
        for h, i, seen in zip(heads, slots, seens):
            growth = lanes([growth_ref[i], growth_ref[i]])
            scaled = growth * seen[:C]
            v = v_ref[0, u * C:(u + 1) * C, h * C:(h + 1) * C].astype(f32)
            rest = lanes([v - scaled[:, :C], -scaled[:, C:]])
            t = t_ref[i]
            freshs.append(mm(lanes([t, t]), rows(split(rest))))
            growths.append(growth)
            yield
        news = []
        for h, i, x, seen, growth, fresh in zip(heads, slots, xs, seens, growths, freshs):
            kh, kl = kend_ref[i, :C], kend_ref[i, C:]
            attend, end = a_ref[i], end_ref[i, :1]
            left = rows([lanes([attend, attend]), lanes([kh, kh]), lanes([kl, jnp.zeros_like(kl)])])
            got = mm(left, rows(split(fresh)))
            out = growth * seen[C:] + got[:C]
            news.append(x * lanes([end, end]) + (got[C:2 * C] + got[2 * C:]))
            o_ref[u * C:(u + 1) * C, h * C:(h + 1) * C] = out[:, :C].astype(o_ref.dtype)
            e_ref[u * C:(u + 1) * C, h * C:(h + 1) * C] = out[:, C:].astype(e_ref.dtype)
            yield
        xs = news
    for h, x in zip(heads, xs):
        x_ref[h] = x


def local_kernel(span, carried, final, length_ref, q_ref, k_ref, v_ref, g_ref, b_ref, *refs):
    index, begin, _ = span
    if carried:
        carry_ref, refs = refs[0], refs[3:]
    o_ref, e_ref, last_ref, x_ref, *kept = refs
    heads = range(x_ref.shape[0])
    step, last = pl.program_id(0), pl.num_programs(0) - 1
    if carried:
        start = [carry_ref[h] for h in heads]
    else:
        start = [(iota((C, 2 * C), 0) + C == iota((C, 2 * C), 1)).astype(f32)] * len(heads)
    chunks = k_ref.shape[1] // C
    first = (begin + jnp.minimum(step, last - 1)) * chunks * C
    lane = iota((len(heads), C), 1)
    g, b = [], []
    for u in range(chunks):
        valid = first + u * C + lane < length_ref[index]
        g.append(jnp.where(valid, g_ref[0, :, u * C:(u + 1) * C], 0.0))
        b.append(jnp.where(valid, b_ref[0, :, u * C:(u + 1) * C], 0.0))
    tasks = [(u, h) for u in range(chunks) for h in heads]
    g, b = rows(g), rows(b)

    def work(chain, fresh):
        ahead = prepare(tasks, q_ref, k_ref, g, b, kept) if fresh else iter(())
        due = 0.0
        if chain:
            for _ in advance(heads, chunks, v_ref, kept, x_ref, o_ref, e_ref, step <= 1, start):
                due += PACE
                while due >= 1.0:
                    next(ahead, None)
                    due -= 1.0
        for _ in ahead:
            pass

    @pl.when(step == 0)
    def _():
        work(False, True)

    @pl.when((step > 0) & (step < last))
    def _():
        work(True, True)

    @pl.when(step == last)
    def _():
        work(True, False)

    @pl.when(step == last)
    def _():
        if final:
            size = last_ref.shape[1] - C
            owners = C // size
            for h in heads:
                shift = x_ref[h, :, :C].T.astype(last_ref.dtype)
                move = x_ref[h, :, C:].T.astype(last_ref.dtype)
                for part in range(owners):
                    last_ref[h * owners + part, :size] = shift[part * size:(part + 1) * size]
                    last_ref[h * owners + part, size:] = move
        else:
            last_ref[...] = x_ref[...]


def local_pass(length, span, q, k, v, g, b, count, carry):
    index, begin, end = span
    _, tokens, width = q.shape
    heads = g.shape[1]
    size = CHUNKS * C
    steps = end - begin
    final = end * size == tokens
    shape = (count, C * heads // count + C, C) if final else (heads, C, 2 * C)
    ahead = pl.BlockSpec((1, size, width), lambda s, _: (index, begin + jnp.minimum(s, steps - 1), 0))
    behind = pl.BlockSpec((1, size, width), lambda s, _: (index, begin + jnp.maximum(s, 1) - 1, 0))
    gate = pl.BlockSpec((1, heads, size), lambda s, _: (index, 0, begin + jnp.minimum(s, steps - 1)))
    out = pl.BlockSpec((size, width), lambda s, _: (begin + jnp.maximum(s, 1) - 1, 0))
    in_specs = [ahead, ahead, behind, gate, gate]
    operands = [length, q, k, v, g, b]
    if carry:
        in_specs += [pl.BlockSpec((heads, C, 2 * C), lambda s, _: (0, 0, 0))] + [pl.BlockSpec(memory_space=pl.ANY)] * 2
        operands += [carry[2], carry[0], carry[1]]
    slots = CHUNKS * heads
    square = pltpu.VMEM((slots, C, C), bf16)
    double = pltpu.VMEM((slots, 2 * C, C), bf16)

    def kernel(*refs):
        local_kernel(span, bool(carry), final, *refs)

    return pl.pallas_call(
        kernel,
        grid_spec=pltpu.PrefetchScalarGridSpec(
            num_scalar_prefetch=1, grid=(steps + 1,),
            in_specs=in_specs,
            out_specs=[out, out, pl.BlockSpec(shape, lambda s, _: (0, 0, 0))],
            scratch_shapes=[pltpu.VMEM((heads, C, 2 * C), f32), double, square, square, double,
                            pltpu.VMEM((slots, C, C), f32), pltpu.VMEM((slots, 8, C), f32)]),
        out_shape=[
            jax.ShapeDtypeStruct((tokens, width), bf16),
            jax.ShapeDtypeStruct((tokens, width), bf16),
            jax.ShapeDtypeStruct(shape, MAP if final else f32)],
        input_output_aliases={7: 0, 8: 1} if carry else {},
        compiler_params=pltpu.CompilerParams(dimension_semantics=("arbitrary",)),
        cost_estimate=pl.CostEstimate(
            flops=20 * steps * size * width * C, bytes_accessed=10 * steps * size * width, transcendentals=0),
        name="local_pass",
    )(*operands)


def prefix_kernel(map_ref, sent_ref):
    count = map_ref.shape[0]
    size = map_ref.shape[1] - C
    own = C // count
    state = jnp.zeros((size, C), f32)
    for i in range(count):
        sent_ref[i, :size] = state.astype(bf16)
        state = mm3(state, map_ref[i, size:].astype(f32)) + map_ref[i, :size].astype(f32)
    for i in range(count):
        first = i * own % size
        for j, x in enumerate(split(state[first:first + own])):
            sent_ref[i, size + j * own:size + (j + 1) * own] = x


def prefix_pass(maps):
    count, depth, _ = maps.shape
    return pl.pallas_call(
        prefix_kernel,
        out_shape=jax.ShapeDtypeStruct((count, depth - C + 2 * (C // count), C), bf16),
        cost_estimate=pl.CostEstimate(flops=1, bytes_accessed=1, transcendentals=0),
        name="prefix_pass",
    )(maps)


def output_pass(scalars, index, o, e, starts, gain, offsets, parts):
    tokens, width = o.shape
    heads = width // C
    owners = starts.shape[0] // heads
    size = C // owners
    depth = tokens // parts
    wide = pl.BlockSpec((depth, width), lambda t, scalar: (scalar[0] ^ (offsets[0] + t), 0))

    def kernel(scalar_ref, o_ref, e_ref, start_ref, gain_ref, *out_refs):
        for i, out_ref in enumerate(out_refs):
            @pl.when(pl.program_id(0) == i)
            def _():
                position = (scalar_ref[0] ^ offsets[i]) * depth + iota((depth, C), 0)
                valid = position < scalar_ref[1 + index]
                gain = gain_ref[...]
                for h in range(heads):
                    part = slice(h * C, (h + 1) * C)
                    o = o_ref[:, part].astype(f32) + mm_nt(e_ref[:, part], rows([start_ref[h * owners + j, :size] for j in range(owners)]))
                    scale = lax.rsqrt(jnp.mean(o * o, axis=1, keepdims=True) + 1e-6)
                    out_ref[:, part] = jnp.where(valid, o * scale * gain, 0.0).astype(bf16)

    return pl.pallas_call(
        kernel,
        grid_spec=pltpu.PrefetchScalarGridSpec(
            num_scalar_prefetch=1, grid=(len(offsets),),
            in_specs=[wide, wide,
                      pl.BlockSpec(starts.shape, lambda t, _: (0, 0, 0)),
                      pl.BlockSpec((1, C), lambda t, _: (0, 0))],
            out_specs=[pl.BlockSpec((depth, width), lambda t, _: (0, 0)) for _ in offsets]),
        out_shape=[jax.ShapeDtypeStruct((depth, width), bf16) for _ in offsets],
        compiler_params=pltpu.CompilerParams(dimension_semantics=("arbitrary",)),
        cost_estimate=pl.CostEstimate(flops=1, bytes_accessed=1, transcendentals=0),
        name="output_pass",
    )(scalars, o, e, starts, gain)


def place_pass(scalars, index, shape, pieces, whole):
    parts = len(pieces)
    width = pieces[0].shape[1]

    def kernel(scalar_ref, *refs):
        out_ref, sems = refs[-2:]
        copies = [pltpu.make_async_copy(
            refs[i],
            out_ref.at[index, :, pl.ds(pl.multiple_of((scalar_ref[0] ^ i) * width, C), width)],
            sems.at[i]) for i in range(parts)]
        for copy in copies:
            copy.start()
        for copy in copies:
            copy.wait()

    aliased = [] if whole is None else [whole]
    return pl.pallas_call(
        kernel,
        in_specs=[pl.BlockSpec(memory_space=pltpu.SMEM)]
        + [pl.BlockSpec(memory_space=pltpu.VMEM) for _ in pieces]
        + [pl.BlockSpec(memory_space=pl.ANY) for _ in aliased],
        out_specs=pl.BlockSpec(memory_space=pl.ANY),
        out_shape=jax.ShapeDtypeStruct(shape, bf16),
        scratch_shapes=[pltpu.SemaphoreType.DMA((parts,))],
        input_output_aliases={1 + parts: 0} if aliased else {},
        cost_estimate=pl.CostEstimate(flops=0, bytes_accessed=4 * parts * pieces[0].size, transcendentals=0),
        name="place_pass",
    )(scalars, *pieces, *aliased)


def after(x, token):
    return x if token is None else lax.optimization_barrier((x, token))[0]


def shards(queries, keys, values, forget_exponent, beta, lengths, norm_gain):
    histories, tokens, width = queries.shape
    heads = forget_exponent.shape[1]
    times = ("grp", "run")
    count = lax.axis_size("grp") * lax.axis_size("run")
    mine = lax.axis_index("grp") * lax.axis_size("run") + lax.axis_index("run")
    parts = lax.axis_size("head")
    owners = count // heads
    length = lengths - mine * tokens
    scalars = jnp.concatenate([lax.axis_index("head")[None], length])
    shape = (histories, tokens // parts, parts * width)
    steps = tokens // (CHUNKS * C)
    half = steps // 2
    gain = norm_gain[None]

    def local(begin, end, carry, token):
        return local_pass(after(length, token), (begin[0], begin[1], end), queries, keys, values,
                          forget_exponent, beta, count, carry)

    def exchange(x):
        return lax.all_to_all(x, times, 0, 0, tiled=True)

    def prefix(maps, token):
        sent = prefix_pass(after(maps, token))
        return sent, exchange(sent)

    def cross(x, r):
        return lax.ppermute(x, "head", [(j, j ^ r) for j in range(parts)])

    def readout(index, part, starts, offsets, token):
        return output_pass(after(scalars, token), index, part[0], part[1], starts, gain, offsets, parts)

    part0 = local((0, 0), steps, None, None)
    maps0 = exchange(part0[2])
    part1 = local((1, 0), half, None, part0[0])
    start, starts0 = prefix(maps0, part1[0])
    part1 = local((1, half), steps, part1, start)
    far = readout(0, part0, starts0, (2, 3), part1[0])
    maps1 = exchange(part1[2])
    far0 = [cross(far[0], 2), cross(far[1], 3)]
    start, starts1 = prefix(maps1, far)
    near = readout(0, part0, starts0, (0, 1), start)
    near0 = [near[0], cross(near[1], 1)]
    far = readout(1, part1, starts1, (2, 3), (near, far0))
    far1 = [cross(far[0], 2), cross(far[1], 3)]
    placed = place_pass(after(scalars, far), 0, shape, near0 + far0, None)
    near = readout(1, part1, starts1, (0, 1), placed)
    near1 = [near[0], cross(near[1], 1)]
    placed = place_pass(scalars, 1, shape, near1 + far1, placed)
    own = C // count
    states = after(jnp.stack([x[:, C // owners:] for x in (starts0, starts1)]), near)
    states = states.reshape(histories, heads, owners, 2, own, C).astype(f32)
    states = lax.dynamic_index_in_dim(states, mine * own * owners // C, 2, keepdims=False)
    return placed, states[:, :, 0] + states[:, :, 1]


def solution(mesh):
    wide = P(None, ("grp", "run"), "head")
    gate = P(None, "head", ("grp", "run"))
    return jax.shard_map(
        shards,
        mesh=mesh,
        in_specs=(wide, wide, wide, gate, gate, P(), P()),
        out_specs=(P(None, ("grp", "run", "head"), None), P(None, "head", ("grp", "run"), None)),
        check_vma=False,
    )
```

```python
import jax
import jax.numpy as jnp
from jax import lax
from jax.experimental import pallas as pl
from jax.experimental.pallas import tpu as pltpu
from jax.sharding import PartitionSpec as P

C = 128
SMALL = 16
f32 = jnp.float32
bf16 = jnp.bfloat16
MAP = bf16
PACE = {2: 2.0, 4: 1.0}
SLABS = 2
SMALL_VMEM = 16 << 20


def mm(a, b):
    return jnp.dot(a, b, preferred_element_type=f32)


def mm_nt(a, b):
    return lax.dot_general(a, b, (((1,), (1,)), ((), ())), preferred_element_type=f32)


def split(x):
    hi = x.astype(bf16)
    return hi, (x - hi.astype(f32)).astype(bf16)


def mm3(a, b):
    ah, al = split(a)
    bh, bl = split(b)
    return mm(jnp.concatenate([ah, al], axis=1), jnp.concatenate([bh, bh], axis=0)) + mm(ah, bl)


def iota(shape, axis):
    return lax.broadcasted_iota(jnp.int32, shape, axis)


def rows(parts):
    return jnp.concatenate(parts, axis=0)


def lanes(parts):
    return jnp.concatenate(parts, axis=1)


def cumulate(g):
    low = (iota((C, C), 0) <= iota((C, C), 1)).astype(f32)
    pad = -g.shape[0] % 8
    if pad:
        g = rows([g, jnp.zeros((pad, C), f32)])
    return jnp.dot(g, low, precision=lax.Precision.HIGHEST, preferred_element_type=f32)


def prepare(tasks, q_ref, k_ref, g, b, kept):
    cum = cumulate(g)
    qk_ref, t_ref, a_ref, kend_ref, growth_ref, end_ref = kept
    row, col = iota((C, C), 0), iota((C, C), 1)
    kbs = []
    for u, h in tasks:
        kf = k_ref[0, u * C:(u + 1) * C, h * C:(h + 1) * C].astype(f32)
        kbs.append((kf * lax.rsqrt(jnp.sum(kf * kf, axis=1, keepdims=True) + 1e-6)).astype(bf16))
        yield
    kts, qks, inners = [], [], []
    for (u, h), kb in zip(tasks, kbs):
        kts.append(kb.T)
        qks.append(rows([kb, q_ref[0, u * C:(u + 1) * C, h * C:(h + 1) * C]]))
        inners.append(mm(qks[-1], kts[-1]))
        yield
    ns, later = [], []
    for i, (inner, kt, qk) in enumerate(zip(inners, kts, qks)):
        one, rate = cum[i:i + 1], b[i:i + 1]
        cr = jnp.broadcast_to(one, (C, C))
        cc = cr.T
        spread = jnp.exp(jnp.where(row >= col, cc - cr, -1e30)) * rate
        ns.append(jnp.where(row > col, inner[:C] * spread, 0.0))
        end = one[:, C - 1:C]
        kend = split(kt.astype(f32) * (rate * jnp.exp(end - one)))
        later.append((qk, (inner[C:] * spread).astype(bf16), kend, jnp.exp(cc), jnp.exp(end)))
        yield
    lane = iota((SMALL, C), 1)
    first = lane // SMALL * SMALL
    packed = []
    for n in ns:
        p = jnp.zeros((SMALL, C), f32)
        for r in range(C // SMALL):
            p = jnp.where(lane // SMALL == r, n[r * SMALL:(r + 1) * SMALL, :], p)
        packed.append(p)
        yield
    ts = [(lane - first == iota((SMALL, C), 0)).astype(f32) for _ in ns]
    for j in range(SMALL - 1):
        columns = [jnp.take_along_axis(p, first + j, axis=1) for p in packed]
        ts = [t - c * t[j:j + 1, :] for t, c in zip(ts, columns)]
        if j % 2 == 1:
            yield
    size = SMALL
    while size < C:
        block = iota((size, C), 1) // size
        count = C // size
        masks = [block == r for r in range(count)]
        zero = jnp.zeros((size, C), bf16)
        ys, halves = [], []
        for n, t in zip(ns, ts):
            low = jnp.zeros((size, C), f32)
            for r in range(0, count, 2):
                low = jnp.where(masks[r], n[(r + 1) * size:(r + 2) * size, :], low)
            th, tl = split(t)
            right = lanes([rows([z for r in range(0, count, 2)
                                 for z in (jnp.where(masks[r], x, jnp.zeros_like(x)), zero)])
                           for x in (th, tl)])
            got = mm(rows(split(low)), right)
            ys.append(got[:size, :C] + (got[:size, C:] + got[size:, :C]))
            halves.append(rows([th, tl]))
            yield
        news = []
        even = block % 2 == 0
        for y, t, half in zip(ys, ts, halves):
            right = lanes([rows([z for r in range(0, count, 2)
                                 for z in (zero, jnp.where(masks[r], x, jnp.zeros_like(x)))])
                           for x in split(y)])
            got = mm(half, right)
            low = got[:size, :C] + (got[:size, C:] + got[size:, :C])
            news.append(rows([jnp.where(even, t, 0.0), jnp.where(even, -low, t)]))
            yield
        ts = news
        size *= 2
    for i, (t, (qk, attend, kend, growth, end)) in enumerate(zip(ts, later)):
        qk_ref[i] = qk
        t_ref[i] = t.astype(bf16)
        a_ref[i] = attend
        kend_ref[i] = rows(kend)
        growth_ref[i] = growth
        end_ref[i] = jnp.broadcast_to(end, (8, C))


def advance(heads, chunks, v_ref, kept, x_ref, o_ref, e_ref, fresh_start, start):
    qk_ref, t_ref, a_ref, kend_ref, growth_ref, end_ref = kept
    xs = [jnp.where(fresh_start, start[h], x_ref[h]) for h in heads]
    for u in range(chunks):
        slots = [u * len(heads) + h for h in heads]
        seens = []
        for i, x in zip(slots, xs):
            qk = qk_ref[i]
            seens.append(mm(lanes([qk, qk]), rows(split(x))))
            yield
        freshs, growths = [], []
        for h, i, seen in zip(heads, slots, seens):
            growth = lanes([growth_ref[i], growth_ref[i]])
            scaled = growth * seen[:C]
            v = v_ref[0, u * C:(u + 1) * C, h * C:(h + 1) * C].astype(f32)
            rest = lanes([v - scaled[:, :C], -scaled[:, C:]])
            t = t_ref[i]
            freshs.append(mm(lanes([t, t]), rows(split(rest))))
            growths.append(growth)
            yield
        news = []
        for h, i, x, seen, growth, fresh in zip(heads, slots, xs, seens, growths, freshs):
            kh, kl = kend_ref[i, :C], kend_ref[i, C:]
            attend, end = a_ref[i], end_ref[i, :1]
            left = rows([lanes([attend, attend]), lanes([kh, kh]), lanes([kl, jnp.zeros_like(kl)])])
            got = mm(left, rows(split(fresh)))
            out = growth * seen[C:] + got[:C]
            news.append(x * lanes([end, end]) + (got[C:2 * C] + got[2 * C:]))
            o_ref[u * C:(u + 1) * C, h * C:(h + 1) * C] = out[:, :C].astype(o_ref.dtype)
            e_ref[u * C:(u + 1) * C, h * C:(h + 1) * C] = out[:, C:].astype(e_ref.dtype)
            yield
        xs = news
    for h, x in zip(heads, xs):
        x_ref[h] = x


def local_kernel(span, carried, final, length_ref, q_ref, k_ref, v_ref, g_ref, b_ref, *refs):
    index, begin, _ = span
    if carried:
        carry_ref, refs = refs[0], refs[3:]
    o_ref, e_ref, last_ref, x_ref, *kept = refs
    heads = range(x_ref.shape[0])
    step, last = pl.program_id(0), pl.num_programs(0) - 1
    if carried:
        start = [carry_ref[h] for h in heads]
    else:
        start = [(iota((C, 2 * C), 0) + C == iota((C, 2 * C), 1)).astype(f32)] * len(heads)
    chunks = k_ref.shape[1] // C
    first = (begin + jnp.minimum(step, last - 1)) * chunks * C
    lane = iota((len(heads), C), 1)
    g, b = [], []
    for u in range(chunks):
        valid = first + u * C + lane < length_ref[index]
        g.append(jnp.where(valid, g_ref[0, :, u * C:(u + 1) * C], 0.0))
        b.append(jnp.where(valid, b_ref[0, :, u * C:(u + 1) * C], 0.0))
    tasks = [(u, h) for u in range(chunks) for h in heads]
    g, b = rows(g), rows(b)

    def work(chain, fresh):
        ahead = prepare(tasks, q_ref, k_ref, g, b, kept) if fresh else iter(())
        due = 0.0
        if chain:
            for _ in advance(heads, chunks, v_ref, kept, x_ref, o_ref, e_ref, step <= 1, start):
                due += PACE[chunks]
                while due >= 1.0:
                    next(ahead, None)
                    due -= 1.0
        for _ in ahead:
            pass

    @pl.when(step == 0)
    def _():
        work(False, True)

    @pl.when((step > 0) & (step < last))
    def _():
        work(True, True)

    @pl.when(step == last)
    def _():
        work(True, False)

    @pl.when(step == last)
    def _():
        if final:
            size = last_ref.shape[1] - C
            owners = C // size
            for h in heads:
                shift = x_ref[h, :, :C].T.astype(last_ref.dtype)
                move = x_ref[h, :, C:].T.astype(last_ref.dtype)
                for part in range(owners):
                    last_ref[h * owners + part, :size] = shift[part * size:(part + 1) * size]
                    last_ref[h * owners + part, size:] = move
        else:
            last_ref[...] = x_ref[...]


def local_pass(length, span, chunks, q, k, v, g, b, count, carry):
    index, begin, end = span
    _, tokens, width = q.shape
    heads = g.shape[1]
    size = chunks * C
    steps = end - begin
    final = end * size == tokens
    shape = (count, C * heads // count + C, C) if final else (heads, C, 2 * C)
    ahead = pl.BlockSpec((1, size, width), lambda s, _: (index, begin + jnp.minimum(s, steps - 1), 0))
    behind = pl.BlockSpec((1, size, width), lambda s, _: (index, begin + jnp.maximum(s, 1) - 1, 0))
    gate = pl.BlockSpec((1, heads, size), lambda s, _: (index, 0, begin + jnp.minimum(s, steps - 1)))
    out = pl.BlockSpec((size, width), lambda s, _: (begin + jnp.maximum(s, 1) - 1, 0))
    in_specs = [ahead, ahead, behind, gate, gate]
    operands = [length, q, k, v, g, b]
    if carry:
        in_specs += [pl.BlockSpec((heads, C, 2 * C), lambda s, _: (0, 0, 0))] + [pl.BlockSpec(memory_space=pl.ANY)] * 2
        operands += [carry[2], carry[0], carry[1]]
    slots = chunks * heads
    square = pltpu.VMEM((slots, C, C), bf16)
    double = pltpu.VMEM((slots, 2 * C, C), bf16)

    def kernel(*refs):
        local_kernel(span, bool(carry), final, *refs)

    return pl.pallas_call(
        kernel,
        grid_spec=pltpu.PrefetchScalarGridSpec(
            num_scalar_prefetch=1, grid=(steps + 1,),
            in_specs=in_specs,
            out_specs=[out, out, pl.BlockSpec(shape, lambda s, _: (0, 0, 0))],
            scratch_shapes=[pltpu.VMEM((heads, C, 2 * C), f32), double, square, square, double,
                            pltpu.VMEM((slots, C, C), f32), pltpu.VMEM((slots, 8, C), f32)]),
        out_shape=[
            jax.ShapeDtypeStruct((tokens, width), bf16),
            jax.ShapeDtypeStruct((tokens, width), bf16),
            jax.ShapeDtypeStruct(shape, MAP if final else f32)],
        input_output_aliases={7: 0, 8: 1} if carry else {},
        compiler_params=pltpu.CompilerParams(dimension_semantics=("arbitrary",)),
        cost_estimate=pl.CostEstimate(
            flops=20 * steps * size * width * C, bytes_accessed=10 * steps * size * width, transcendentals=0),
        name="local_pass",
    )(*operands)


def prefix_kernel(map_ref, sent_ref):
    count = map_ref.shape[0]
    size = map_ref.shape[1] - C
    own = C // count
    state = jnp.zeros((size, C), f32)
    for i in range(count):
        sent_ref[i, :size] = state.astype(bf16)
        state = mm3(state, map_ref[i, size:].astype(f32)) + map_ref[i, :size].astype(f32)
    for i in range(count):
        first = i * own % size
        for j, x in enumerate(split(state[first:first + own])):
            sent_ref[i, size + j * own:size + (j + 1) * own] = x


def prefix_pass(maps):
    count, depth, _ = maps.shape
    return pl.pallas_call(
        prefix_kernel,
        out_shape=jax.ShapeDtypeStruct((count, depth - C + 2 * (C // count), C), bf16),
        cost_estimate=pl.CostEstimate(flops=1, bytes_accessed=1, transcendentals=0),
        compiler_params=pltpu.CompilerParams(vmem_limit_bytes=SMALL_VMEM),
        name="prefix_pass",
    )(maps)


def output_pass(scalars, index, o, e, starts, gain, offsets, parts):
    tokens, width = o.shape
    heads = width // C
    owners = starts.shape[0] // heads
    size = C // owners
    depth = tokens // parts
    slab = depth // SLABS
    wide = pl.BlockSpec((slab, width), lambda t, u, scalar: ((scalar[0] ^ (offsets[0] + t)) * SLABS + u, 0))

    def kernel(scalar_ref, o_ref, e_ref, start_ref, gain_ref, *out_refs):
        begin = pl.multiple_of(pl.program_id(1) * slab, slab)
        position = (scalar_ref[0] ^ (offsets[0] + pl.program_id(0))) * depth + begin + iota((slab, C), 0)
        valid = position < scalar_ref[1 + index]
        gain = gain_ref[...]
        cuts = [slice(h * C, (h + 1) * C) for h in range(heads)]
        starts = [rows([start_ref[h * owners + j, :size] for j in range(owners)]) for h in range(heads)]
        outs = [mm_nt(e_ref[:, cut], start) for cut, start in zip(cuts, starts)]
        outs = [o_ref[:, cut].astype(f32) + x for cut, x in zip(cuts, outs)]
        means = [jnp.mean(x * x, axis=1, keepdims=True) for x in outs]
        scales = [lax.rsqrt(x + 1e-6) for x in means]
        outs = [jnp.where(valid, x * scale * gain, 0.0).astype(bf16) for x, scale in zip(outs, scales)]
        for i, out_ref in enumerate(out_refs):
            @pl.when(pl.program_id(0) == i)
            def _():
                for cut, x in zip(cuts, outs):
                    out_ref[pl.ds(begin, slab), cut] = x

    return pl.pallas_call(
        kernel,
        grid_spec=pltpu.PrefetchScalarGridSpec(
            num_scalar_prefetch=1, grid=(len(offsets), SLABS),
            in_specs=[wide, wide,
                      pl.BlockSpec(starts.shape, lambda t, u, _: (0, 0, 0)),
                      pl.BlockSpec((1, C), lambda t, u, _: (0, 0))],
            out_specs=[pl.BlockSpec((depth, width), lambda t, u, _: (0, 0)) for _ in offsets]),
        out_shape=[jax.ShapeDtypeStruct((depth, width), bf16) for _ in offsets],
        compiler_params=pltpu.CompilerParams(
            dimension_semantics=("arbitrary", "arbitrary"), vmem_limit_bytes=SMALL_VMEM),
        cost_estimate=pl.CostEstimate(flops=1, bytes_accessed=1, transcendentals=0),
        name="output_pass",
    )(scalars, o, e, starts, gain)


def place_pass(scalars, index, shape, pieces, whole):
    parts = len(pieces)
    width = pieces[0].shape[1]

    def kernel(scalar_ref, *refs):
        out_ref, sems = refs[-2:]
        copies = [pltpu.make_async_copy(
            refs[i],
            out_ref.at[index, :, pl.ds(pl.multiple_of((scalar_ref[0] ^ i) * width, C), width)],
            sems.at[i]) for i in range(parts)]
        for copy in copies:
            copy.start()
        for copy in copies:
            copy.wait()

    aliased = [] if whole is None else [whole]
    return pl.pallas_call(
        kernel,
        in_specs=[pl.BlockSpec(memory_space=pltpu.SMEM)]
        + [pl.BlockSpec(memory_space=pltpu.VMEM) for _ in pieces]
        + [pl.BlockSpec(memory_space=pl.ANY) for _ in aliased],
        out_specs=pl.BlockSpec(memory_space=pl.ANY),
        out_shape=jax.ShapeDtypeStruct(shape, bf16),
        scratch_shapes=[pltpu.SemaphoreType.DMA((parts,))],
        input_output_aliases={1 + parts: 0} if aliased else {},
        cost_estimate=pl.CostEstimate(flops=0, bytes_accessed=4 * parts * pieces[0].size, transcendentals=0),
        compiler_params=pltpu.CompilerParams(vmem_limit_bytes=SMALL_VMEM),
        name="place_pass",
    )(scalars, *pieces, *aliased)


def after(x, token):
    return x if token is None else lax.optimization_barrier((x, token))[0]


def shards(queries, keys, values, forget_exponent, beta, lengths, norm_gain):
    histories, tokens, width = queries.shape
    heads = forget_exponent.shape[1]
    times = ("grp", "run")
    count = lax.axis_size("grp") * lax.axis_size("run")
    mine = lax.axis_index("grp") * lax.axis_size("run") + lax.axis_index("run")
    parts = lax.axis_size("head")
    owners = count // heads
    length = lengths - mine * tokens
    scalars = jnp.concatenate([lax.axis_index("head")[None], length])
    shape = (histories, tokens // parts, parts * width)
    half = tokens // (2 * C) // 2
    gain = norm_gain[None]

    def local(span, chunks, carry, token):
        return local_pass(after(length, token), span, chunks, queries, keys, values,
                          forget_exponent, beta, count, carry)

    def exchange(x):
        return lax.all_to_all(x, times, 0, 0, tiled=True)

    def prefix(maps, token):
        sent = prefix_pass(after(maps, token))
        return sent, exchange(sent)

    def cross(x, r):
        return lax.ppermute(x, "head", [(j, j ^ r) for j in range(parts)])

    def readout(index, part, starts, offsets, token):
        return output_pass(after(scalars, token), index, part[0], part[1], starts, gain, offsets, parts)

    part0 = local((0, 0, tokens // (4 * C)), 4, None, None)
    maps0 = exchange(part0[2])
    part1 = local((1, 0, half), 2, None, part0[0])
    start, starts0 = prefix(maps0, part1[0])
    part1 = local((1, half, 2 * half), 2, part1, start)
    far = readout(0, part0, starts0, (2, 3), part1[0])
    maps1 = exchange(part1[2])
    far0 = [cross(far[0], 2), cross(far[1], 3)]
    start, starts1 = prefix(maps1, far)
    far = readout(1, part1, starts1, (2, 3), (start, far0))
    far1 = [cross(far[0], 2), cross(far[1], 3)]
    near = readout(0, part0, starts0, (0, 1), far)
    near0 = [near[0], cross(near[1], 1)]
    near = readout(1, part1, starts1, (0, 1), near)
    near1 = [near[0], cross(near[1], 1)]
    placed = place_pass(after(scalars, near), 0, shape, near0 + far0, None)
    placed = place_pass(scalars, 1, shape, near1 + far1, placed)
    own = C // count
    states = after(jnp.stack([x[:, C // owners:] for x in (starts0, starts1)]), near)
    states = states.reshape(histories, heads, owners, 2, own, C).astype(f32)
    states = lax.dynamic_index_in_dim(states, mine * own * owners // C, 2, keepdims=False)
    return placed, states[:, :, 0] + states[:, :, 1]


def solution(mesh):
    wide = P(None, ("grp", "run"), "head")
    gate = P(None, "head", ("grp", "run"))
    return jax.shard_map(
        shards,
        mesh=mesh,
        in_specs=(wide, wide, wide, gate, gate, P(), P()),
        out_specs=(P(None, ("grp", "run", "head"), None), P(None, "head", ("grp", "run"), None)),
        check_vma=False,
    )
```

```python
import jax
import jax.numpy as jnp
from jax import lax
from jax.experimental import pallas as pl
from jax.experimental.pallas import tpu as pltpu
from jax.sharding import PartitionSpec as P

C = 128
SMALL = 16
f32 = jnp.float32
bf16 = jnp.bfloat16
MAP = bf16
PACE = {2: 2.0, 4: 1.0}
SMALL_VMEM = 16 << 20
LARGE_VMEM = 60 << 20


def mm(a, b):
    return jnp.dot(a, b, preferred_element_type=f32)


def mm_nt(a, b):
    return lax.dot_general(a, b, (((1,), (1,)), ((), ())), preferred_element_type=f32)


def split(x):
    hi = x.astype(bf16)
    return hi, (x - hi.astype(f32)).astype(bf16)


def mm3(a, b):
    ah, al = split(a)
    bh, bl = split(b)
    return mm(jnp.concatenate([ah, al], axis=1), jnp.concatenate([bh, bh], axis=0)) + mm(ah, bl)


def iota(shape, axis):
    return lax.broadcasted_iota(jnp.int32, shape, axis)


def rows(parts):
    return jnp.concatenate(parts, axis=0)


def lanes(parts):
    return jnp.concatenate(parts, axis=1)


def cumulate(g):
    low = (iota((C, C), 0) <= iota((C, C), 1)).astype(f32)
    pad = -g.shape[0] % 8
    if pad:
        g = rows([g, jnp.zeros((pad, C), f32)])
    return jnp.dot(g, low, precision=lax.Precision.HIGHEST, preferred_element_type=f32)


def prepare(tasks, q_ref, k_ref, g, b, kept):
    cum = cumulate(g)
    qk_ref, t_ref, a_ref, kend_ref, growth_ref, end_ref = kept
    row, col = iota((C, C), 0), iota((C, C), 1)
    kbs = []
    for u, h in tasks:
        kf = k_ref[0, u * C:(u + 1) * C, h * C:(h + 1) * C].astype(f32)
        kbs.append((kf * lax.rsqrt(jnp.sum(kf * kf, axis=1, keepdims=True) + 1e-6)).astype(bf16))
        yield
    kts, qks, inners = [], [], []
    for (u, h), kb in zip(tasks, kbs):
        kts.append(kb.T)
        qks.append(rows([kb, q_ref[0, u * C:(u + 1) * C, h * C:(h + 1) * C]]))
        inners.append(mm(qks[-1], kts[-1]))
        yield
    ns, later = [], []
    for i, (inner, kt, qk) in enumerate(zip(inners, kts, qks)):
        one, rate = cum[i:i + 1], b[i:i + 1]
        cr = jnp.broadcast_to(one, (C, C))
        cc = cr.T
        spread = jnp.exp(jnp.where(row >= col, cc - cr, -1e30)) * rate
        ns.append(jnp.where(row > col, inner[:C] * spread, 0.0))
        end = one[:, C - 1:C]
        kend = split(kt.astype(f32) * (rate * jnp.exp(end - one)))
        later.append((qk, (inner[C:] * spread).astype(bf16), kend, jnp.exp(cc), jnp.exp(end)))
        yield
    lane = iota((SMALL, C), 1)
    first = lane // SMALL * SMALL
    packed = []
    for n in ns:
        p = jnp.zeros((SMALL, C), f32)
        for r in range(C // SMALL):
            p = jnp.where(lane // SMALL == r, n[r * SMALL:(r + 1) * SMALL, :], p)
        packed.append(p)
        yield
    ts = [(lane - first == iota((SMALL, C), 0)).astype(f32) for _ in ns]
    for j in range(SMALL - 1):
        columns = [jnp.take_along_axis(p, first + j, axis=1) for p in packed]
        ts = [t - c * t[j:j + 1, :] for t, c in zip(ts, columns)]
        if j % 2 == 1:
            yield
    size = SMALL
    while size < C:
        block = iota((size, C), 1) // size
        count = C // size
        masks = [block == r for r in range(count)]
        zero = jnp.zeros((size, C), bf16)
        ys, halves = [], []
        for n, t in zip(ns, ts):
            low = jnp.zeros((size, C), f32)
            for r in range(0, count, 2):
                low = jnp.where(masks[r], n[(r + 1) * size:(r + 2) * size, :], low)
            th, tl = split(t)
            right = lanes([rows([z for r in range(0, count, 2)
                                 for z in (jnp.where(masks[r], x, jnp.zeros_like(x)), zero)])
                           for x in (th, tl)])
            got = mm(rows(split(low)), right)
            ys.append(got[:size, :C] + (got[:size, C:] + got[size:, :C]))
            halves.append(rows([th, tl]))
            yield
        news = []
        even = block % 2 == 0
        for y, t, half in zip(ys, ts, halves):
            right = lanes([rows([z for r in range(0, count, 2)
                                 for z in (zero, jnp.where(masks[r], x, jnp.zeros_like(x)))])
                           for x in split(y)])
            got = mm(half, right)
            low = got[:size, :C] + (got[:size, C:] + got[size:, :C])
            news.append(rows([jnp.where(even, t, 0.0), jnp.where(even, -low, t)]))
            yield
        ts = news
        size *= 2
    for i, (t, (qk, attend, kend, growth, end)) in enumerate(zip(ts, later)):
        qk_ref[i] = qk
        t_ref[i] = t.astype(bf16)
        a_ref[i] = attend
        kend_ref[i] = rows(kend)
        growth_ref[i] = growth
        end_ref[i] = jnp.broadcast_to(end, (8, C))


def advance(heads, chunks, v_ref, kept, x_ref, o_ref, e_ref, fresh_start, start):
    qk_ref, t_ref, a_ref, kend_ref, growth_ref, end_ref = kept
    xs = [jnp.where(fresh_start, start[h], x_ref[h]) for h in heads]
    for u in range(chunks):
        slots = [u * len(heads) + h for h in heads]
        seens = []
        for i, x in zip(slots, xs):
            qk = qk_ref[i]
            seens.append(mm(lanes([qk, qk]), rows(split(x))))
            yield
        freshs, growths = [], []
        for h, i, seen in zip(heads, slots, seens):
            growth = lanes([growth_ref[i], growth_ref[i]])
            scaled = growth * seen[:C]
            v = v_ref[0, u * C:(u + 1) * C, h * C:(h + 1) * C].astype(f32)
            rest = lanes([v - scaled[:, :C], -scaled[:, C:]])
            t = t_ref[i]
            freshs.append(mm(lanes([t, t]), rows(split(rest))))
            growths.append(growth)
            yield
        news = []
        for h, i, x, seen, growth, fresh in zip(heads, slots, xs, seens, growths, freshs):
            kh, kl = kend_ref[i, :C], kend_ref[i, C:]
            attend, end = a_ref[i], end_ref[i, :1]
            left = rows([lanes([attend, attend]), lanes([kh, kh]), lanes([kl, jnp.zeros_like(kl)])])
            got = mm(left, rows(split(fresh)))
            out = growth * seen[C:] + got[:C]
            news.append(x * lanes([end, end]) + (got[C:2 * C] + got[2 * C:]))
            o_ref[u * C:(u + 1) * C, h * C:(h + 1) * C] = out[:, :C].astype(o_ref.dtype)
            e_ref[u * C:(u + 1) * C, h * C:(h + 1) * C] = out[:, C:].astype(e_ref.dtype)
            yield
        xs = news
    for h, x in zip(heads, xs):
        x_ref[h] = x


def local_kernel(span, carried, final, length_ref, q_ref, k_ref, v_ref, g_ref, b_ref, *refs):
    index, begin, _ = span
    if carried:
        carry_ref, refs = refs[0], refs[3:]
    o_ref, e_ref, last_ref, x_ref, *kept = refs
    heads = range(x_ref.shape[0])
    step, last = pl.program_id(0), pl.num_programs(0) - 1
    if carried:
        start = [carry_ref[h] for h in heads]
    else:
        start = [(iota((C, 2 * C), 0) + C == iota((C, 2 * C), 1)).astype(f32)] * len(heads)
    chunks = k_ref.shape[1] // C
    first = (begin + jnp.minimum(step, last - 1)) * chunks * C
    lane = iota((len(heads), C), 1)
    g, b = [], []
    for u in range(chunks):
        valid = first + u * C + lane < length_ref[index]
        g.append(jnp.where(valid, g_ref[0, :, u * C:(u + 1) * C], 0.0))
        b.append(jnp.where(valid, b_ref[0, :, u * C:(u + 1) * C], 0.0))
    tasks = [(u, h) for u in range(chunks) for h in heads]
    g, b = rows(g), rows(b)

    def work(chain, fresh):
        ahead = prepare(tasks, q_ref, k_ref, g, b, kept) if fresh else iter(())
        due = 0.0
        if chain:
            for _ in advance(heads, chunks, v_ref, kept, x_ref, o_ref, e_ref, step <= 1, start):
                due += PACE[chunks]
                while due >= 1.0:
                    next(ahead, None)
                    due -= 1.0
        for _ in ahead:
            pass

    @pl.when(step == 0)
    def _():
        work(False, True)

    @pl.when((step > 0) & (step < last))
    def _():
        work(True, True)

    @pl.when(step == last)
    def _():
        work(True, False)

    @pl.when(step == last)
    def _():
        if final:
            size = last_ref.shape[1] - C
            owners = C // size
            for h in heads:
                shift = x_ref[h, :, :C].T.astype(last_ref.dtype)
                move = x_ref[h, :, C:].T.astype(last_ref.dtype)
                for part in range(owners):
                    last_ref[h * owners + part, :size] = shift[part * size:(part + 1) * size]
                    last_ref[h * owners + part, size:] = move
        else:
            last_ref[...] = x_ref[...]


def local_pass(length, span, chunks, q, k, v, g, b, count, carry):
    index, begin, end = span
    _, tokens, width = q.shape
    heads = g.shape[1]
    size = chunks * C
    steps = end - begin
    final = end * size == tokens
    shape = (count, C * heads // count + C, C) if final else (heads, C, 2 * C)
    ahead = pl.BlockSpec((1, size, width), lambda s, _: (index, begin + jnp.minimum(s, steps - 1), 0))
    behind = pl.BlockSpec((1, size, width), lambda s, _: (index, begin + jnp.maximum(s, 1) - 1, 0))
    gate = pl.BlockSpec((1, heads, size), lambda s, _: (index, 0, begin + jnp.minimum(s, steps - 1)))
    out = pl.BlockSpec((size, width), lambda s, _: (begin + jnp.maximum(s, 1) - 1, 0))
    in_specs = [ahead, ahead, behind, gate, gate]
    operands = [length, q, k, v, g, b]
    if carry:
        in_specs += [pl.BlockSpec((heads, C, 2 * C), lambda s, _: (0, 0, 0))] + [pl.BlockSpec(memory_space=pl.ANY)] * 2
        operands += [carry[2], carry[0], carry[1]]
    slots = chunks * heads
    square = pltpu.VMEM((slots, C, C), bf16)
    double = pltpu.VMEM((slots, 2 * C, C), bf16)

    def kernel(*refs):
        local_kernel(span, bool(carry), final, *refs)

    return pl.pallas_call(
        kernel,
        grid_spec=pltpu.PrefetchScalarGridSpec(
            num_scalar_prefetch=1, grid=(steps + 1,),
            in_specs=in_specs,
            out_specs=[out, out, pl.BlockSpec(shape, lambda s, _: (0, 0, 0))],
            scratch_shapes=[pltpu.VMEM((heads, C, 2 * C), f32), double, square, square, double,
                            pltpu.VMEM((slots, C, C), f32), pltpu.VMEM((slots, 8, C), f32)]),
        out_shape=[
            jax.ShapeDtypeStruct((tokens, width), bf16),
            jax.ShapeDtypeStruct((tokens, width), bf16),
            jax.ShapeDtypeStruct(shape, MAP if final else f32)],
        input_output_aliases={7: 0, 8: 1} if carry else {},
        compiler_params=pltpu.CompilerParams(dimension_semantics=("arbitrary",)),
        cost_estimate=pl.CostEstimate(
            flops=20 * steps * size * width * C, bytes_accessed=10 * steps * size * width, transcendentals=0),
        name="local_pass",
    )(*operands)


def prefix_kernel(map_ref, sent_ref):
    count = map_ref.shape[0]
    size = map_ref.shape[1] - C
    own = C // count
    state = jnp.zeros((size, C), f32)
    for i in range(count):
        sent_ref[i, :size] = state.astype(bf16)
        state = mm3(state, map_ref[i, size:].astype(f32)) + map_ref[i, :size].astype(f32)
    for i in range(count):
        first = i * own % size
        for j, x in enumerate(split(state[first:first + own])):
            sent_ref[i, size + j * own:size + (j + 1) * own] = x


def prefix_pass(maps):
    count, depth, _ = maps.shape
    return pl.pallas_call(
        prefix_kernel,
        out_shape=jax.ShapeDtypeStruct((count, depth - C + 2 * (C // count), C), bf16),
        cost_estimate=pl.CostEstimate(flops=1, bytes_accessed=1, transcendentals=0),
        compiler_params=pltpu.CompilerParams(vmem_limit_bytes=SMALL_VMEM),
        name="prefix_pass",
    )(maps)


def output_pass(scalars, index, o, e, starts, gain, offsets, parts, vmem):
    tokens, width = o.shape
    heads = width // C
    owners = starts.shape[0] // heads
    size = C // owners
    depth = tokens // parts
    slabs = 1 if vmem == LARGE_VMEM else 2
    slab = depth // slabs
    wide = pl.BlockSpec((slab, width), lambda t, u, scalar: ((scalar[0] ^ (offsets[0] + t)) * slabs + u, 0))

    def kernel(scalar_ref, o_ref, e_ref, start_ref, gain_ref, *out_refs):
        begin = pl.multiple_of(pl.program_id(1) * slab, slab)
        position = (scalar_ref[0] ^ (offsets[0] + pl.program_id(0))) * depth + begin + iota((slab, C), 0)
        valid = position < scalar_ref[1 + index]
        gain = gain_ref[...]
        cuts = [slice(h * C, (h + 1) * C) for h in range(heads)]
        starts = [rows([start_ref[h * owners + j, :size] for j in range(owners)]) for h in range(heads)]
        outs = [mm_nt(e_ref[:, cut], start) for cut, start in zip(cuts, starts)]
        outs = [o_ref[:, cut].astype(f32) + x for cut, x in zip(cuts, outs)]
        means = [jnp.mean(x * x, axis=1, keepdims=True) for x in outs]
        scales = [lax.rsqrt(x + 1e-6) for x in means]
        outs = [jnp.where(valid, x * scale * gain, 0.0).astype(bf16) for x, scale in zip(outs, scales)]
        for i, out_ref in enumerate(out_refs):
            @pl.when(pl.program_id(0) == i)
            def _():
                for cut, x in zip(cuts, outs):
                    out_ref[pl.ds(begin, slab), cut] = x

    return pl.pallas_call(
        kernel,
        grid_spec=pltpu.PrefetchScalarGridSpec(
            num_scalar_prefetch=1, grid=(len(offsets), slabs),
            in_specs=[wide, wide,
                      pl.BlockSpec(starts.shape, lambda t, u, _: (0, 0, 0)),
                      pl.BlockSpec((1, C), lambda t, u, _: (0, 0))],
            out_specs=[pl.BlockSpec((depth, width), lambda t, u, _: (0, 0)) for _ in offsets]),
        out_shape=[jax.ShapeDtypeStruct((depth, width), bf16) for _ in offsets],
        compiler_params=pltpu.CompilerParams(
            dimension_semantics=("arbitrary", "arbitrary"), vmem_limit_bytes=vmem),
        cost_estimate=pl.CostEstimate(flops=1, bytes_accessed=1, transcendentals=0),
        name="output_pass",
    )(scalars, o, e, starts, gain)


def place_pass(scalars, index, shape, pieces, whole):
    parts = len(pieces)
    width = pieces[0].shape[1]

    def kernel(scalar_ref, *refs):
        out_ref, sems = refs[-2:]
        copies = [pltpu.make_async_copy(
            refs[i],
            out_ref.at[index, :, pl.ds(pl.multiple_of((scalar_ref[0] ^ i) * width, C), width)],
            sems.at[i]) for i in range(parts)]
        for copy in copies:
            copy.start()
        for copy in copies:
            copy.wait()

    aliased = [] if whole is None else [whole]
    return pl.pallas_call(
        kernel,
        in_specs=[pl.BlockSpec(memory_space=pltpu.SMEM)]
        + [pl.BlockSpec(memory_space=pltpu.VMEM) for _ in pieces]
        + [pl.BlockSpec(memory_space=pl.ANY) for _ in aliased],
        out_specs=pl.BlockSpec(memory_space=pl.ANY),
        out_shape=jax.ShapeDtypeStruct(shape, bf16),
        scratch_shapes=[pltpu.SemaphoreType.DMA((parts,))],
        input_output_aliases={1 + parts: 0} if aliased else {},
        cost_estimate=pl.CostEstimate(flops=0, bytes_accessed=4 * parts * pieces[0].size, transcendentals=0),
        compiler_params=pltpu.CompilerParams(vmem_limit_bytes=SMALL_VMEM),
        name="place_pass",
    )(scalars, *pieces, *aliased)


def after(x, token):
    return x if token is None else lax.optimization_barrier((x, token))[0]


def shards(queries, keys, values, forget_exponent, beta, lengths, norm_gain):
    histories, tokens, width = queries.shape
    heads = forget_exponent.shape[1]
    times = ("grp", "run")
    count = lax.axis_size("grp") * lax.axis_size("run")
    mine = lax.axis_index("grp") * lax.axis_size("run") + lax.axis_index("run")
    parts = lax.axis_size("head")
    owners = count // heads
    length = lengths - mine * tokens
    scalars = jnp.concatenate([lax.axis_index("head")[None], length])
    shape = (histories, tokens // parts, parts * width)
    half = tokens // (2 * C) // 2
    gain = norm_gain[None]

    def local(span, chunks, carry, token):
        return local_pass(after(length, token), span, chunks, queries, keys, values,
                          forget_exponent, beta, count, carry)

    def exchange(x):
        return lax.all_to_all(x, times, 0, 0, tiled=True)

    def prefix(maps, token):
        sent = prefix_pass(after(maps, token))
        return sent, exchange(sent)

    def cross(x, r):
        return lax.ppermute(x, "head", [(j, j ^ r) for j in range(parts)])

    def readout(index, part, starts, offsets, token, vmem=SMALL_VMEM):
        return output_pass(after(scalars, token), index, part[0], part[1], starts, gain, offsets, parts, vmem)

    part0 = local((0, 0, tokens // (4 * C)), 4, None, None)
    maps0 = exchange(part0[2])
    part1 = local((1, 0, half), 2, None, part0[0])
    start, starts0 = prefix(maps0, part1[0])
    part1 = local((1, half, 2 * half), 2, part1, start)
    far = readout(0, part0, starts0, (2, 3), part1[0], LARGE_VMEM)
    maps1 = exchange(part1[2])
    far0 = [cross(far[0], 2), cross(far[1], 3)]
    start, starts1 = prefix(maps1, far)
    far = readout(1, part1, starts1, (2, 3), (start, far0))
    far1 = [cross(far[0], 2), cross(far[1], 3)]
    near = readout(0, part0, starts0, (0, 1), far)
    near0 = [near[0], cross(near[1], 1)]
    near = readout(1, part1, starts1, (0, 1), near)
    near1 = [near[0], cross(near[1], 1)]
    placed = place_pass(after(scalars, near), 0, shape, near0 + far0, None)
    placed = place_pass(scalars, 1, shape, near1 + far1, placed)
    own = C // count
    states = after(jnp.stack([x[:, C // owners:] for x in (starts0, starts1)]), near)
    states = states.reshape(histories, heads, owners, 2, own, C).astype(f32)
    states = lax.dynamic_index_in_dim(states, mine * own * owners // C, 2, keepdims=False)
    return placed, states[:, :, 0] + states[:, :, 1]


def solution(mesh):
    wide = P(None, ("grp", "run"), "head")
    gate = P(None, "head", ("grp", "run"))
    return jax.shard_map(
        shards,
        mesh=mesh,
        in_specs=(wide, wide, wide, gate, gate, P(), P()),
        out_specs=(P(None, ("grp", "run", "head"), None), P(None, "head", ("grp", "run"), None)),
        check_vma=False,
    )
```
